32 devices in a mesh: dp: 8 (over z, y), sub: 4 (over x, core).
Axes of the slice: x: 2, y: 2, z: 4, core: 2. Of those that a mesh axis runs over, the one named last changes fastest.
Arguments:
- queries: bfloat16 [32, 64, 576], P('dp'), may hold values from -195 to 195
- own_cache: bfloat16 [32, 1024, 576], P('dp', 'sub'), may hold values from -8 to 8
- own_len: int32 [32, 4], P('dp', 'sub'), may hold values from 2 to 256
- host_cache: bfloat16 [8, 4, 8, 1024, 576], P('dp', 'sub'), may hold values from -8 to 8
- host_len: int32 [8, 4, 8], P('dp', 'sub'), may hold values from 2 to 1024
- page_plan: int32 [8, 4, 8], P('dp', 'sub'), may hold values from 0 to 3
- value_up: bfloat16 [64, 512, 128], P('sub'), may hold values from -0.25 to 0.25
Outputs:
- attended: bfloat16 [32, 64, 128], P('dp', 'sub')
The draws below stay inside these ranges and needn't reach their ends.
All inputs are finite; a program needn't handle non-finite values.
Results may differ from the reference program's by a relative error of at most 0.008.
Values may be sent and summed in bfloat16 or wider, within the bound.
No kernel may reach another device: no remote copies, remote signals or barrier semaphores. Data moves between devices by JAX's collectives and lax.ppermute only.
A program may use at most 128 MiB of HBM per device.

```python
import jax
import jax.numpy as jnp
from jax import lax

H = 64
DL = 512
DR = 64
VD = 128
RG = 4
OWN_TOK = 256
HOST_TOK = 1024
B = 32
N_DP = 8
N_SUB = 4


def draw_page_plan(key, part):
    base = jax.random.fold_in(key, 11)
    earlier = jax.random.randint(jax.random.fold_in(base, 1), (N_DP, N_SUB, N_DP), 0, RG)
    later = jax.random.randint(jax.random.fold_in(base, 2), (N_DP, N_SUB, N_DP), 0, RG)
    ranked = jnp.minimum(earlier, later).astype(jnp.int32)
    ranks = jax.random.randint(jax.random.fold_in(base, 3), (N_DP, N_SUB, RG), 0, 1 << 20) * RG
    ranks = ranks + lax.broadcasted_iota(jnp.int32, (N_DP, N_SUB, RG), 2)
    ordering = jnp.argsort(ranks, axis=-1, stable=True).astype(jnp.int32)
    return jnp.take_along_axis(ordering, ranked, axis=-1).astype(jnp.int32)


def draw_queries(key, part):
    base = jax.random.fold_in(key, 31)
    values = jax.random.truncated_normal(jax.random.fold_in(base, 1), -4.0, 4.0, (N_DP * RG, H, DL + DR), jnp.float32)
    return values.astype(jnp.bfloat16)


def draw_own_cache(key, part):
    base = jax.random.fold_in(key, 21)
    noise = jax.random.truncated_normal(jax.random.fold_in(base, 1), -4.0, 4.0, (N_DP * RG, N_SUB, OWN_TOK, DL + DR), jnp.float32)
    centre = jax.random.truncated_normal(jax.random.fold_in(base, 2), -4.0, 4.0, (N_DP * RG, N_SUB, 1, DL), jnp.float32)
    latent = noise[..., :DL] + centre
    rotary = noise[..., DL:]
    whole = jnp.concatenate([latent, rotary], axis=-1)
    return whole.reshape(N_DP * RG, N_SUB * OWN_TOK, DL + DR).astype(jnp.bfloat16)


def draw_host_cache(key, part):
    base = jax.random.fold_in(key, 41)

    def one_helper(helper):
        inner = jax.random.fold_in(base, helper)
        noise = jax.random.truncated_normal(jax.random.fold_in(inner, 1), -4.0, 4.0, (N_SUB, N_DP, HOST_TOK, DL + DR), jnp.float32)
        centre = jax.random.truncated_normal(jax.random.fold_in(inner, 2), -4.0, 4.0, (N_SUB, N_DP, 1, DL), jnp.float32)
        latent = noise[..., :DL] + centre
        rotary = noise[..., DL:]
        return jnp.concatenate([latent, rotary], axis=-1).astype(jnp.bfloat16)
    return lax.map(one_helper, jnp.arange(N_DP, dtype=jnp.int32))


def place_ends(array, key, low, high):
    index_at = [jax.random.randint(jax.random.fold_in(key, axis), (), 0, length) for axis, length in enumerate(array.shape)]
    widest = array.shape.index(max(array.shape))
    neighbour = index_at[:widest] + [(index_at[widest] + 1) % array.shape[widest]] + index_at[widest + 1:]
    return array.at[tuple(index_at)].set(low).at[tuple(neighbour)].set(high)


def shard_levels(own_key, shape, shards, least, high):
    loudness = 1.0
    for dim, parts in shards:
        steps = jax.random.uniform(jax.random.fold_in(jax.random.fold_in(own_key, 6), dim), (parts,), jnp.float32, least / len(shards), high / len(shards))
        loudness = loudness * jnp.repeat(jnp.exp(steps), shape[dim] // parts).reshape((-1,) + (1,) * (len(shape) - 1 - dim))
    return loudness


def normal_values(key, extent, spread, most, pieces=(), kind=jnp.bfloat16):
    values = spread * jax.random.normal(key, extent, jnp.float32)
    if pieces:
        values = values * shard_levels(key, extent, pieces, -0.22, 0.18)
    return jnp.clip(values, -most, most).astype(kind)


def setup_inputs(seed: int = 0) -> dict:
    seeds = jax.random.split(jax.random.key(seed), 8)
    return {
        "queries": draw_queries(jax.random.fold_in(seeds[7], 71), 0),
        "own_cache": draw_own_cache(jax.random.fold_in(seeds[7], 71), 0),
        "own_len": place_ends(jax.random.randint(seeds[2], (B, N_SUB), 2, OWN_TOK + 1), jax.random.fold_in(seeds[2], 1), 2, OWN_TOK).astype(jnp.int32),
        "host_cache": draw_host_cache(jax.random.fold_in(seeds[7], 71), 0),
        "host_len": place_ends(jax.random.randint(seeds[4], (N_DP, N_SUB, N_DP), 2, HOST_TOK + 1), jax.random.fold_in(seeds[4], 1), 2, HOST_TOK).astype(jnp.int32),
        "page_plan": draw_page_plan(jax.random.fold_in(seeds[7], 71), 0),
        "value_up": normal_values(seeds[6], (H, DL, VD), DL ** -0.5, 0.25, ((0, 4),)),
    }


score_scale = 192 ** -0.5
masked_score = -1e30
highest = lax.Precision.HIGHEST


def attend(queries, slot_cache, lengths):
    query_wide = queries.astype(jnp.float32)
    cache_wide = slot_cache.astype(jnp.float32)
    scores = jnp.einsum("phd,ptd->pht", query_wide, cache_wide, precision=highest) * score_scale
    position = jnp.arange(slot_cache.shape[1], dtype=jnp.int32)
    scores = jnp.where(position[None, None, :] < lengths[:, None, None], scores, masked_score)
    largest = jnp.max(scores, axis=2, keepdims=True)
    exponent = jnp.exp(scores - largest)
    totals = jnp.sum(exponent, axis=2)
    weights = lax.optimization_barrier(exponent.astype(jnp.bfloat16)).astype(jnp.float32)
    weighted = jnp.einsum("pht,ptd->phd", weights, cache_wide[:, :, :DL], precision=highest)
    return weighted / totals[:, :, None], largest[:, :, 0] + jnp.log(totals)


def reference(queries, own_cache, own_len, host_cache, host_len, page_plan, value_up):
    width = DL + DR
    own_groups = own_cache.reshape(N_DP, RG * N_SUB, OWN_TOK, width)
    query_groups = queries.reshape(N_DP, RG, H, width)
    length_groups = own_len.reshape(N_DP, RG * N_SUB)

    def own_block(operands):
        group_queries, group_cache, group_lengths = operands
        return attend(jnp.repeat(group_queries, N_SUB, axis=0), group_cache, group_lengths)

    own_out, own_lse = lax.map(own_block, (query_groups, own_groups, length_groups))
    own_out = own_out.reshape(N_DP, RG, N_SUB, H, DL)
    own_lse = own_lse.reshape(N_DP, RG, N_SUB, H)
    owners = jnp.arange(N_DP, dtype=jnp.int32) * RG

    def host_block(operands):
        slot_cache, slot_lengths, slot_plan = operands
        index = (owners[None, :] + slot_plan).reshape(N_SUB * N_DP).astype(jnp.int32)
        return attend(queries[index], slot_cache.reshape(N_SUB * N_DP, HOST_TOK, width), slot_lengths.reshape(N_SUB * N_DP))

    plan_by_helper = jnp.transpose(page_plan, (2, 1, 0))
    host_out, host_lse = lax.map(host_block, (host_cache, host_len, plan_by_helper))
    host_out = jnp.transpose(host_out.reshape(N_DP, N_SUB, N_DP, H, DL), (2, 1, 0, 3, 4))
    host_lse = jnp.transpose(host_lse.reshape(N_DP, N_SUB, N_DP, H), (2, 1, 0, 3))
    matched = page_plan[..., None] == jnp.arange(RG, dtype=jnp.int32)
    masked = jnp.where(matched[..., None], host_lse[:, :, :, None, :], masked_score)
    largest = jnp.maximum(jnp.max(own_lse, axis=2), jnp.max(masked, axis=(1, 2)))
    own_weight = jnp.exp(own_lse - largest[:, :, None, :])
    help_weight = jnp.exp(masked - largest[:, None, None, :, :])
    summed = jnp.einsum("grsh,grshd->grhd", own_weight, own_out, precision=highest)
    summed = summed + jnp.einsum("gsprh,gsphd->grhd", help_weight, host_out, precision=highest)
    totals = jnp.sum(own_weight, axis=2) + jnp.sum(help_weight, axis=(1, 2))
    latent = (summed / totals[..., None]).astype(jnp.bfloat16).reshape(N_DP * RG, H, DL)
    result = jnp.einsum("bhd,hde->bhe", latent.astype(jnp.float32), value_up.astype(jnp.float32), precision=highest)
    return result.astype(jnp.bfloat16)
```

```python
import functools

import jax
import jax.numpy as jnp
from jax import lax
from jax.experimental import pallas as pl
from jax.experimental.pallas import tpu as pltpu
from jax.sharding import PartitionSpec as P

DL = 512
LANES = 128
TILES = DL // LANES
PIECE = 32
PLAN_LANE = 96
score_scale = 192 ** (-0.5)
masked_score = -1e30


VMEM = pl.BlockSpec(memory_space=pltpu.VMEM)
SMEM = pl.BlockSpec(memory_space=pltpu.SMEM)


def lane_index(shape):
    return lax.broadcasted_iota(jnp.int32, shape, len(shape) - 1)


def pack_query_kernel(targets, plan_ref, query_ref, *outs):
    me = lax.axis_index("dp")
    heads = query_ref.shape[1]
    half = heads // 2
    for k, out in zip(targets, outs):
        r = plan_ref[me ^ k]
        for i in range(TILES):
            out[i * heads:(i + 1) * heads, :] = query_ref[r, :, i * LANES:(i + 1) * LANES]
        rotary = query_ref[r, :, DL:]
        out[TILES * heads:, :] = jnp.concatenate([rotary[:half], rotary[half:]], axis=1)


def unpack_query(packed_ref, heads):
    latent = jnp.concatenate(
        [packed_ref[i * heads:(i + 1) * heads, :] for i in range(TILES)], axis=1
    )
    tail = packed_ref[TILES * heads:, :]
    rotary = jnp.concatenate([tail[:, : LANES // 2], tail[:, LANES // 2:]], axis=0)
    return latent, rotary


def attend(latent, rotary, keys, length):
    width = keys.shape[1]
    scores = jnp.dot(latent, keys[:DL, :], preferred_element_type=jnp.float32)
    scores = scores + jnp.dot(rotary, keys[DL:, :], preferred_element_type=jnp.float32)
    scores = scores * score_scale
    scores = jnp.where(lane_index((1, width)) < length, scores, masked_score)
    largest = jnp.max(scores, axis=1, keepdims=True)
    exponent = jnp.exp(scores - largest)
    totals = jnp.sum(exponent, axis=1, keepdims=True)
    weights = exponent.astype(jnp.bfloat16)
    weighted = lax.dot_general(
        weights, keys[:DL, :], (((1,), (1,)), ((), ())), preferred_element_type=jnp.float32
    )
    return weighted / totals, largest + jnp.log(totals)


def put_lane(block, lane, column):
    return jnp.where(lane_index(block.shape) == lane, column, block)


def split_three(block):
    high = block.astype(jnp.bfloat16).astype(jnp.float32)
    rest = block - high
    middle = rest.astype(jnp.bfloat16).astype(jnp.float32)
    low = rest - middle
    return high + pltpu.roll(middle, PIECE, 1) + pltpu.roll(low, 2 * PIECE, 1)


def join_three(block):
    return block + pltpu.roll(block, LANES - PIECE, 1) + pltpu.roll(block, LANES - 2 * PIECE, 1)


def put_slot(stage, slot, rows, partial):
    heads = partial.shape[0]
    for i in range(TILES):
        stage[i, pl.ds(slot, heads, stride=rows), :] = partial[:, i * LANES:(i + 1) * LANES]


def write_messages(stage, side, rows, outs, head_part):
    me = lax.axis_index("sub")
    for k, out in enumerate(outs):
        part = me ^ k
        start = pl.multiple_of(part * (head_part * rows), 8)
        for i in range(TILES):
            chunk = stage[i, pl.ds(start, head_part * rows), :]
            out[i * head_part * rows:(i + 1) * head_part * rows, :] = chunk.astype(jnp.bfloat16)
        side_start = pl.multiple_of(part * head_part, 8)
        out[TILES * head_part * rows:, :] = side[pl.ds(side_start, head_part), :].astype(jnp.bfloat16)


def near_kernel(near, rows, n_sub, plan_ref, own_len_ref, host_len_ref, query_ref, own_ref, host_ref, *refs):
    packed, outs, (stage, side) = refs[: near - 1], refs[near - 1: near - 1 + n_sub], refs[near - 1 + n_sub:]
    me = lax.axis_index("dp")
    requests, heads, _ = query_ref.shape
    groups = host_ref.shape[0]
    table = jnp.zeros((heads, LANES), jnp.float32)
    for r in range(requests):
        query = query_ref[r]
        partial, lse = attend(query[:, :DL], query[:, DL:], own_ref.at[r], own_len_ref[r])
        put_slot(stage, r, rows, partial)
        table = put_lane(table, r, lse)
    for k in range(near):
        g = me ^ k
        if k == 0:
            query = query_ref[plan_ref[me]]
            latent, rotary = query[:, :DL], query[:, DL:]
        else:
            latent, rotary = unpack_query(packed[k - 1], heads)
        partial, lse = attend(latent, rotary, host_ref.at[g], host_len_ref[g])
        put_slot(stage, requests + k, rows, partial)
        table = put_lane(table, requests + k, lse)
    table = split_three(table)
    for p in range(groups):
        table = put_lane(table, PLAN_LANE + p, plan_ref[p].astype(jnp.float32))
    side[...] = table
    write_messages(stage, side, rows, outs, heads // n_sub)


def far_kernel(near, rows, n_sub, host_len_ref, host_ref, *refs):
    groups = host_ref.shape[0]
    far = groups - near
    packed, outs, (stage, side) = refs[:far], refs[far: far + n_sub], refs[far + n_sub:]
    me = lax.axis_index("dp")
    heads = side.shape[0]
    table = jnp.zeros((heads, LANES), jnp.float32)
    if rows != far:
        stage[...] = jnp.zeros_like(stage)
    for j in range(far):
        g = me ^ (near + j)
        latent, rotary = unpack_query(packed[j], heads)
        partial, lse = attend(latent, rotary, host_ref.at[g], host_len_ref[g])
        put_slot(stage, j, rows, partial)
        table = put_lane(table, j, lse)
    side[...] = split_three(table)
    write_messages(stage, side, rows, outs, heads // n_sub)


def lift_kernel(near, requests, near_rows, far_rows, n_sub, groups, value_ref, *refs):
    near_in, far_in = refs[:n_sub], refs[n_sub: 2 * n_sub]
    out, own_out, own_side, lhs, lifted = refs[2 * n_sub:]
    me = lax.axis_index("dp")
    part = value_ref.shape[0]
    near_block, far_block = max(near_rows, 8), max(far_rows, 8)
    seats = n_sub * part
    for h in range(part):
        offset = 0
        for sources, rows, block in ((near_in, near_rows, near_block), (far_in, far_rows, far_block)):
            start = h * rows // block * block
            for source in sources:
                for i in range(TILES):
                    base = i * part * rows + start
                    lhs[h, offset: offset + block, i * LANES:(i + 1) * LANES] = source[base: base + block, :]
                offset += block
        result = jnp.dot(lhs[h], value_ref[h], preferred_element_type=jnp.float32)
        for s in range(n_sub):
            base = s * near_block
            lifted[pl.ds(s * part + h, near_block, stride=seats), :] = result[base: base + near_block]
            base = n_sub * near_block + s * far_block
            piece = result[base: base + far_block]
            skip = h * far_rows % far_block
            if skip:
                piece = pltpu.roll(piece, far_block - skip, 0)
            lifted[pl.ds(near_block * seats + s * part + h, far_block, stride=seats), :] = piece
    side_near = [ref[TILES * part * near_rows:, :].astype(jnp.float32) for ref in near_in]
    side_far = [ref[TILES * part * far_rows:, :].astype(jnp.float32) for ref in far_in]
    lane = lane_index((part, LANES))
    for k in range(groups):
        g = me ^ k
        row = requests + k if k < near else k - near
        first = (row if k < near else near_block + row) * seats
        out[g, :seats, :] = lifted[first: first + seats, :].astype(jnp.bfloat16)
        tile = jnp.zeros((part, LANES), jnp.float32)
        for s in range(n_sub):
            source = side_near[s] if k < near else side_far[s]
            moved = pltpu.roll(source, (s - row) % LANES, 1) if s != row else source
            tile = jnp.where((lane % PIECE == s) & (lane < 3 * PIECE), moved, tile)
        out[g, seats:, :] = tile.astype(jnp.bfloat16)
    own_out[...] = lifted[: requests * seats, :]
    for s in range(n_sub):
        own_side[s] = side_near[s]


def finish_kernel(requests, n_sub, groups, back_ref, own_ref, side_ref, out_ref):
    part = out_ref.shape[1]
    seats = n_sub * part
    lane = lane_index((part, LANES))
    sides = [side_ref[s] for s in range(n_sub)]
    joined = [join_three(side) for side in sides]
    help_lse, help_plan = [], []
    for p in range(groups):
        help_lse.append(join_three(back_ref[p, seats:, :].astype(jnp.float32)))
        plan = jnp.full((part, LANES), -1.0, jnp.float32)
        for s in range(n_sub):
            plan = put_lane(plan, s, sides[s][:, PLAN_LANE + p: PLAN_LANE + p + 1])
        help_plan.append(plan)
    weights = []
    peaks = []
    owns = []
    for r in range(requests):
        own = jnp.full((part, LANES), masked_score, jnp.float32)
        for s in range(n_sub):
            own = put_lane(own, s, joined[s][:, r: r + 1])
        peak = own
        for p in range(groups):
            peak = jnp.maximum(peak, jnp.where(help_plan[p] == r, help_lse[p], masked_score))
        peaks.append(jnp.max(peak, axis=1, keepdims=True))
        owns.append(own)
    for r in range(requests):
        own_weight = jnp.where(lane < n_sub, jnp.exp(owns[r] - peaks[r]), 0.0)
        total = own_weight
        summed = jnp.zeros((part, LANES), jnp.float32)
        for s in range(n_sub):
            first = (r * n_sub + s) * part
            summed = summed + own_weight[:, s: s + 1] * own_ref[first: first + part, :]
        for p in range(groups):
            chosen = help_plan[p] == r
            weight = jnp.exp(jnp.where(chosen, help_lse[p] - peaks[r], masked_score))
            total = total + weight
            for s in range(n_sub):
                value = back_ref[p, s * part:(s + 1) * part, :].astype(jnp.float32)
                summed = summed + weight[:, s: s + 1] * value
        total = jnp.sum(total, axis=1, keepdims=True)
        out_ref[r] = (summed / total).astype(jnp.bfloat16)


def exchange(array, axis, k):
    size = lax.axis_size(axis)
    return lax.ppermute(array, axis, [(i, i ^ k) for i in range(size)])


def call(kernel, outs, in_specs, scratch=(), limit=None, cost=None):
    return pl.pallas_call(
        kernel,
        out_shape=outs,
        in_specs=in_specs,
        out_specs=jax.tree.map(lambda _: VMEM, outs),
        scratch_shapes=list(scratch),
        compiler_params=pltpu.CompilerParams(vmem_limit_bytes=limit),
        cost_estimate=cost,
    )


def local(queries, own_cache, own_len, host_cache, host_len, page_plan, value_up):
    groups, n_sub = lax.axis_size("dp"), lax.axis_size("sub")
    requests, heads, width = queries.shape
    part = heads // n_sub
    slot_tokens = host_cache.shape[3]
    near = min(4, groups)
    far = groups - near
    near_rows = requests + near
    far_rows = far if far in (1, 2, 4) else -(-far // 8) * 8
    plan = page_plan.reshape(groups)
    lengths = host_len.reshape(groups)
    own_lengths = own_len.reshape(requests)
    own_keys = jnp.swapaxes(own_cache, 1, 2)
    host_keys = jnp.swapaxes(host_cache.reshape(groups, slot_tokens, width), 1, 2)

    targets = list(range(1, groups))
    shape = jax.ShapeDtypeStruct((heads * width // LANES, LANES), jnp.bfloat16)
    outgoing = call(
        functools.partial(pack_query_kernel, targets), [shape] * len(targets), [SMEM, VMEM], limit=4 << 20
    )(plan, queries)
    order = list(range(near, groups)) + list(range(1, near))
    received = {k: exchange(outgoing[k - 1], "dp", k) for k in order}

    def message(rows):
        return jax.ShapeDtypeStruct((TILES * part * rows + part, LANES), jnp.bfloat16)

    def stages(rows):
        return [pltpu.VMEM((TILES, heads * rows, LANES), jnp.float32), pltpu.VMEM((heads, LANES), jnp.float32)]

    def cost(slots):
        return pl.CostEstimate(
            flops=2 * slots * heads * slot_tokens * (width + DL),
            bytes_accessed=2 * slots * slot_tokens * width,
            transcendentals=slots * heads * slot_tokens,
        )

    near_out = call(
        functools.partial(near_kernel, near, near_rows, n_sub),
        [message(near_rows)] * n_sub,
        [SMEM] * 3 + [VMEM] * (3 + near - 1),
        stages(near_rows),
        limit=None,
        cost=cost(near + 1),
    )(plan, own_lengths, lengths, queries, own_keys, host_keys, *[received[k] for k in range(1, near)])
    far_out = call(
        functools.partial(far_kernel, near, far_rows, n_sub),
        [message(far_rows)] * n_sub,
        [SMEM] + [VMEM] * (1 + far),
        stages(far_rows),
        limit=None,
        cost=cost(far),
    )(lengths, host_keys, *[received[k] for k in range(near, groups)])
    sub_order = [k for k in range(2, n_sub)] + [1]
    near_in, far_in = {0: near_out[0]}, {0: far_out[0]}
    for k in sub_order:
        near_in[k] = exchange(near_out[k], "sub", k)
    for k in sub_order:
        far_in[k] = exchange(far_out[k], "sub", k)

    near_block, far_block = max(near_rows, 8), max(far_rows, 8)
    seats = n_sub * part
    back, own, side = call(
        functools.partial(lift_kernel, near, requests, near_rows, far_rows, n_sub, groups),
        [
            jax.ShapeDtypeStruct((groups, seats + part, LANES), jnp.bfloat16),
            jax.ShapeDtypeStruct((requests * seats, LANES), jnp.float32),
            jax.ShapeDtypeStruct((n_sub, part, LANES), jnp.float32),
        ],
        [VMEM] * (1 + 2 * n_sub),
        [
            pltpu.VMEM((part, n_sub * (near_block + far_block), DL), jnp.bfloat16),
            pltpu.VMEM(((near_block + far_block) * seats, LANES), jnp.float32),
        ],
        limit=None,
    )(value_up, *[near_in[k] for k in range(n_sub)], *[far_in[k] for k in range(n_sub)])
    back = lax.all_to_all(back, "dp", split_axis=0, concat_axis=0, tiled=True)
    return call(
        functools.partial(finish_kernel, requests, n_sub, groups),
        jax.ShapeDtypeStruct((requests, part, LANES), jnp.bfloat16),
        [VMEM] * 3,
        limit=None,
    )(back, own, side)


def solution(mesh):
    return jax.shard_map(
        local,
        mesh=mesh,
        in_specs=(
            P("dp", None, None),
            P("dp", "sub", None),
            P("dp", "sub"),
            P("dp", "sub", None, None, None),
            P("dp", "sub", None),
            P("dp", "sub", None),
            P("sub", None, None),
        ),
        out_specs=P("dp", "sub", None),
        check_vma=False,
    )
```

```python
import functools

import jax
import jax.numpy as jnp
from jax import lax
from jax.experimental import pallas as pl
from jax.experimental.pallas import tpu as pltpu
from jax.sharding import PartitionSpec as P


DL = 512
LANES = 128
TILES = DL // LANES
PIECE = 32
PLAN_LANE = 96
score_scale = 192 ** (-0.5)
masked_score = -1e30


OWN_LIMIT = 42 << 20
PACK_LIMIT = 64_000_000
KERNEL_LIMIT = 14 << 20

VMEM = pl.BlockSpec(memory_space=pltpu.VMEM)
SMEM = pl.BlockSpec(memory_space=pltpu.SMEM)
HBM = pl.BlockSpec(memory_space=pltpu.HBM)


def lane_index(shape):
    return lax.broadcasted_iota(jnp.int32, shape, len(shape) - 1)


def pack_query_kernel(targets, plan_hbm, query_hbm, *refs):
    outs, (plan_ref, query_ref, sems) = refs[:-3], refs[-3:]
    plan_copy = pltpu.make_async_copy(plan_hbm, plan_ref, sems.at[0])
    query_copy = pltpu.make_async_copy(query_hbm, query_ref, sems.at[1])
    plan_copy.start()
    query_copy.start()
    me = lax.axis_index("dp")
    heads = query_ref.shape[1]
    half = heads // 2
    plan_copy.wait()
    query_copy.wait()
    for k, out in zip(targets, outs):
        r = plan_ref[me ^ k]
        for i in range(TILES):
            out[i * heads:(i + 1) * heads, :] = query_ref[r, :, i * LANES:(i + 1) * LANES]
        rotary = query_ref[r, :, DL:]
        out[TILES * heads:, :] = jnp.concatenate([rotary[:half], rotary[half:]], axis=1)


def unpack_query(packed_ref, heads):
    latent = jnp.concatenate(
        [packed_ref[i * heads:(i + 1) * heads, :] for i in range(TILES)], axis=1
    )
    tail = packed_ref[TILES * heads:, :]
    rotary = jnp.concatenate([tail[:, : LANES // 2], tail[:, LANES // 2:]], axis=0)
    return latent, rotary


def attend(latent, rotary, keys, length):
    width = keys.shape[1]
    scores = jnp.dot(latent, keys[:DL, :], preferred_element_type=jnp.float32)
    scores = scores + jnp.dot(rotary, keys[DL:, :], preferred_element_type=jnp.float32)
    scores = scores * score_scale
    scores = jnp.where(lane_index((1, width)) < length, scores, masked_score)
    largest = jnp.max(scores, axis=1, keepdims=True)
    exponent = jnp.exp(scores - largest)
    totals = jnp.sum(exponent, axis=1, keepdims=True)
    weights = exponent.astype(jnp.bfloat16)
    weighted = lax.dot_general(
        weights, keys[:DL, :], (((1,), (1,)), ((), ())), preferred_element_type=jnp.float32
    )
    return weighted / totals, largest + jnp.log(totals)


def put_lane(block, lane, column):
    return jnp.where(lane_index(block.shape) == lane, column, block)


def split_three(block):
    high = block.astype(jnp.bfloat16).astype(jnp.float32)
    rest = block - high
    middle = rest.astype(jnp.bfloat16).astype(jnp.float32)
    low = rest - middle
    return high + pltpu.roll(middle, PIECE, 1) + pltpu.roll(low, 2 * PIECE, 1)


def join_three(block):
    return block + pltpu.roll(block, LANES - PIECE, 1) + pltpu.roll(block, LANES - 2 * PIECE, 1)


def put_slot(stage, slot, rows, partial):
    heads = partial.shape[0]
    for i in range(TILES):
        stage[i, pl.ds(slot, heads, stride=rows), :] = partial[:, i * LANES:(i + 1) * LANES]


def write_messages(stage, side, rows, outs, part, other=None, taken=0):
    me = lax.axis_index("sub")
    for k, out in enumerate(outs):
        seat = me ^ k
        start = pl.multiple_of(seat * (part * rows), 8)
        for i in range(TILES):
            chunk = stage[i, pl.ds(start, part * rows), :]
            if taken:
                row = lax.broadcasted_iota(jnp.int32, chunk.shape, 0) % rows
                chunk = jnp.where(row < taken, other[i, pl.ds(start, part * rows), :], chunk)
            out[i * part * rows:(i + 1) * part * rows, :] = chunk.astype(jnp.bfloat16)
        side_start = pl.multiple_of(seat * part, 8)
        out[TILES * part * rows:, :] = side[pl.ds(side_start, part), :].astype(jnp.bfloat16)


def own_kernel(rows, plan_ref, own_len_ref, host_len_ref, query_ref, own_ref, host_ref, cache_ref, stage, table_ref, sems):
    me = lax.axis_index("dp")
    requests, heads, _ = query_ref.shape
    groups = host_ref.shape[0]
    copies = []
    for k in range(groups):
        g = me ^ k
        copies.append(pltpu.make_async_copy(host_ref.at[g], cache_ref.at[g], sems.at[k]))
        copies[k].start()
    table = jnp.zeros((heads, LANES), jnp.float32)
    for r in range(requests):
        query = query_ref[r]
        partial, lse = attend(query[:, :DL], query[:, DL:], own_ref.at[r], own_len_ref[r])
        put_slot(stage, r, rows, partial)
        table = put_lane(table, r, lse)
    copies[0].wait()
    query = query_ref[plan_ref[me]]
    partial, lse = attend(query[:, :DL], query[:, DL:], cache_ref.at[me], host_len_ref[me])
    put_slot(stage, requests, rows, partial)
    table = put_lane(table, requests, lse)
    for p in range(groups):
        table = put_lane(table, PLAN_LANE + p, plan_ref[p].astype(jnp.float32))
    table_ref[...] = table
    for copy in copies[1:]:
        copy.wait()


def near_kernel(near, requests, rows, n_sub, host_len_ref, host_ref, own_stage, table_ref, *refs):
    packed, outs, (stage, side) = refs[: near - 1], refs[near - 1: near - 1 + n_sub], refs[near - 1 + n_sub:]
    me = lax.axis_index("dp")
    heads = side.shape[0]
    table = table_ref[...]
    lane = lane_index(table.shape)
    for k in range(1, near):
        g = me ^ k
        latent, rotary = unpack_query(packed[k - 1], heads)
        partial, lse = attend(latent, rotary, host_ref.at[g], host_len_ref[g])
        put_slot(stage, requests + k, rows, partial)
        table = put_lane(table, requests + k, lse)
    pieces = split_three(jnp.where(lane < PIECE, table, 0.0))
    side[...] = jnp.where(lane < PLAN_LANE, pieces, table)
    write_messages(stage, side, rows, outs, heads // n_sub, own_stage, requests + 1)


def far_kernel(near, rows, n_sub, host_len_ref, host_ref, *refs):
    groups = host_ref.shape[0]
    far = groups - near
    packed, outs, (stage, side) = refs[:far], refs[far: far + n_sub], refs[far + n_sub:]
    me = lax.axis_index("dp")
    heads = side.shape[0]
    table = jnp.zeros((heads, LANES), jnp.float32)
    if rows != far:
        stage[...] = jnp.zeros_like(stage)
    for j in range(far):
        g = me ^ (near + j)
        latent, rotary = unpack_query(packed[j], heads)
        partial, lse = attend(latent, rotary, host_ref.at[g], host_len_ref[g])
        put_slot(stage, j, rows, partial)
        table = put_lane(table, j, lse)
    side[...] = split_three(table)
    write_messages(stage, side, rows, outs, heads // n_sub)


def lift_kernel(near, requests, near_rows, far_rows, n_sub, groups, value_ref, *refs):
    near_in, far_in = refs[:n_sub], refs[n_sub: 2 * n_sub]
    out, own_out, own_side, lhs, lifted = refs[2 * n_sub:]
    me = lax.axis_index("dp")
    part = value_ref.shape[0]
    near_block, far_block = max(near_rows, 8), max(far_rows, 8)
    seats = n_sub * part
    for h in range(part):
        offset = 0
        for sources, rows, block in ((near_in, near_rows, near_block), (far_in, far_rows, far_block)):
            start = h * rows // block * block
            for source in sources:
                for i in range(TILES):
                    base = i * part * rows + start
                    lhs[h, offset: offset + block, i * LANES:(i + 1) * LANES] = source[base: base + block, :]
                offset += block
        result = jnp.dot(lhs[h], value_ref[h], preferred_element_type=jnp.float32)
        for s in range(n_sub):
            base = s * near_block
            lifted[pl.ds(s * part + h, near_block, stride=seats), :] = result[base: base + near_block]
            base = n_sub * near_block + s * far_block
            piece = result[base: base + far_block]
            skip = h * far_rows % far_block
            if skip:
                piece = pltpu.roll(piece, far_block - skip, 0)
            lifted[pl.ds(near_block * seats + s * part + h, far_block, stride=seats), :] = piece
    side_near = [ref[TILES * part * near_rows:, :].astype(jnp.float32) for ref in near_in]
    side_far = [ref[TILES * part * far_rows:, :].astype(jnp.float32) for ref in far_in]
    lane = lane_index((part, LANES))
    for k in range(groups):
        g = me ^ k
        row = requests + k if k < near else k - near
        first = (row if k < near else near_block + row) * seats
        out[g, :seats, :] = lifted[first: first + seats, :].astype(jnp.bfloat16)
        tile = jnp.zeros((part, LANES), jnp.float32)
        for s in range(n_sub):
            source = side_near[s] if k < near else side_far[s]
            moved = pltpu.roll(source, (s - row) % LANES, 1) if s != row else source
            tile = jnp.where((lane % PIECE == s) & (lane < 3 * PIECE), moved, tile)
        out[g, seats:, :] = tile.astype(jnp.bfloat16)
    own_out[...] = lifted[: requests * seats, :]
    for s in range(n_sub):
        own_side[s] = side_near[s]


def finish_kernel(requests, n_sub, groups, back_ref, own_ref, side_ref, out_ref):
    part = out_ref.shape[1]
    seats = n_sub * part
    lane = lane_index((part, LANES))
    sides = [side_ref[s] for s in range(n_sub)]
    joined = [join_three(side) for side in sides]
    help_lse, help_plan = [], []
    for p in range(groups):
        help_lse.append(join_three(back_ref[p, seats:, :].astype(jnp.float32)))
        plan = jnp.full((part, LANES), -1.0, jnp.float32)
        for s in range(n_sub):
            plan = put_lane(plan, s, sides[s][:, PLAN_LANE + p: PLAN_LANE + p + 1])
        help_plan.append(plan)
    peaks = []
    owns = []
    for r in range(requests):
        own = jnp.full((part, LANES), masked_score, jnp.float32)
        for s in range(n_sub):
            own = put_lane(own, s, joined[s][:, r: r + 1])
        peak = own
        for p in range(groups):
            peak = jnp.maximum(peak, jnp.where(help_plan[p] == r, help_lse[p], masked_score))
        peaks.append(jnp.max(peak, axis=1, keepdims=True))
        owns.append(own)
    for r in range(requests):
        own_weight = jnp.where(lane < n_sub, jnp.exp(owns[r] - peaks[r]), 0.0)
        total = own_weight
        summed = jnp.zeros((part, LANES), jnp.float32)
        for s in range(n_sub):
            first = (r * n_sub + s) * part
            summed = summed + own_weight[:, s: s + 1] * own_ref[first: first + part, :]
        for p in range(groups):
            chosen = help_plan[p] == r
            weight = jnp.exp(jnp.where(chosen, help_lse[p] - peaks[r], masked_score))
            total = total + weight
            for s in range(n_sub):
                value = back_ref[p, s * part:(s + 1) * part, :].astype(jnp.float32)
                summed = summed + weight[:, s: s + 1] * value
        total = jnp.sum(total, axis=1, keepdims=True)
        out_ref[r] = (summed / total).astype(jnp.bfloat16)


def exchange(array, axis, k):
    size = lax.axis_size(axis)
    return lax.ppermute(array, axis, [(i, i ^ k) for i in range(size)])


def call(kernel, outs, in_specs, scratch=(), limit=None, cost=None):
    def run(*args):
        return pl.pallas_call(
            kernel,
            out_shape=outs,
            in_specs=in_specs,
            out_specs=jax.tree.map(lambda _: VMEM, outs),
            scratch_shapes=list(scratch),
            compiler_params=pltpu.CompilerParams(vmem_limit_bytes=limit),
            cost_estimate=cost,
        )(*args)

    return run


def near_count(groups):
    return min(4, groups)


def local(queries, own_cache, own_len, host_cache, host_len, page_plan, value_up):
    groups, n_sub = lax.axis_size("dp"), lax.axis_size("sub")
    requests, heads, width = queries.shape
    part = heads // n_sub
    slot_tokens = host_cache.shape[3]
    near = near_count(groups)
    far = groups - near
    near_rows = requests + near
    far_rows = far if far in (1, 2, 4) else -(-far // 8) * 8
    plan = page_plan.reshape(groups)
    lengths = host_len.reshape(groups)
    own_lengths = own_len.reshape(requests)
    own_keys = jnp.swapaxes(own_cache, 1, 2)
    host_keys = jnp.swapaxes(host_cache.reshape(groups, slot_tokens, width), 1, 2)

    targets = list(range(1, groups))
    packed = jax.ShapeDtypeStruct((heads * width // LANES, LANES), jnp.bfloat16)
    outgoing = call(
        functools.partial(pack_query_kernel, targets), [packed] * len(targets), [HBM, HBM],
        [pltpu.SMEM(plan.shape, plan.dtype), pltpu.VMEM(queries.shape, queries.dtype), pltpu.SemaphoreType.DMA((2,))],
        limit=PACK_LIMIT,
    )(plan, queries)
    order = list(range(near, groups)) + list(range(1, near))
    received = {k: exchange(outgoing[k - 1], "dp", k) for k in order}

    def message(rows):
        return jax.ShapeDtypeStruct((TILES * part * rows + part, LANES), jnp.bfloat16)

    def stage_shape(rows):
        return (TILES, heads * rows, LANES)

    def stages(rows):
        return [pltpu.VMEM(stage_shape(rows), jnp.float32), pltpu.VMEM((heads, LANES), jnp.float32)]

    def cost(slots):
        return pl.CostEstimate(
            flops=2 * slots * heads * slot_tokens * (width + DL),
            bytes_accessed=2 * slots * slot_tokens * width,
            transcendentals=slots * heads * slot_tokens,
        )

    cache, own_stage, table = call(
        functools.partial(own_kernel, near_rows),
        [
            jax.ShapeDtypeStruct(host_keys.shape, host_keys.dtype),
            jax.ShapeDtypeStruct(stage_shape(near_rows), jnp.float32),
            jax.ShapeDtypeStruct((heads, LANES), jnp.float32),
        ],
        [SMEM] * 3 + [VMEM] * 2 + [HBM],
        [pltpu.SemaphoreType.DMA((groups,))],
        limit=OWN_LIMIT,
        cost=cost(groups),
    )(plan, own_lengths, lengths, queries, own_keys, host_keys)
    near_out = call(
        functools.partial(near_kernel, near, requests, near_rows, n_sub),
        [message(near_rows)] * n_sub,
        [SMEM] + [VMEM] * (3 + near - 1),
        stages(near_rows),
        limit=KERNEL_LIMIT,
        cost=cost(near - 1),
    )(lengths, cache, own_stage, table, *[received[k] for k in range(1, near)])
    far_out = call(
        functools.partial(far_kernel, near, far_rows, n_sub),
        [message(far_rows)] * n_sub,
        [SMEM] + [VMEM] * (1 + far),
        stages(far_rows),
        limit=KERNEL_LIMIT,
        cost=cost(far),
    )(lengths, cache, *[received[k] for k in range(near, groups)])
    sub_order = [k for k in range(2, n_sub)] + [1]
    near_in, far_in = {0: near_out[0]}, {0: far_out[0]}
    for k in sub_order:
        near_in[k] = exchange(near_out[k], "sub", k)
    for k in sub_order:
        far_in[k] = exchange(far_out[k], "sub", k)

    near_block, far_block = max(near_rows, 8), max(far_rows, 8)
    seats = n_sub * part
    back, own, side = call(
        functools.partial(lift_kernel, near, requests, near_rows, far_rows, n_sub, groups),
        [
            jax.ShapeDtypeStruct((groups, seats + part, LANES), jnp.bfloat16),
            jax.ShapeDtypeStruct((requests * seats, LANES), jnp.float32),
            jax.ShapeDtypeStruct((n_sub, part, LANES), jnp.float32),
        ],
        [VMEM] * (1 + 2 * n_sub),
        [
            pltpu.VMEM((part, n_sub * (near_block + far_block), DL), jnp.bfloat16),
            pltpu.VMEM(((near_block + far_block) * seats, LANES), jnp.float32),
        ],
        limit=12 << 20,
    )(value_up, *[near_in[k] for k in range(n_sub)], *[far_in[k] for k in range(n_sub)])
    back = lax.all_to_all(back, "dp", split_axis=0, concat_axis=0, tiled=True)
    return call(
        functools.partial(finish_kernel, requests, n_sub, groups),
        jax.ShapeDtypeStruct((requests, part, LANES), jnp.bfloat16),
        [VMEM] * 3,
        limit=4 << 20,
    )(back, own, side)


def solution(mesh):
    return jax.shard_map(
        local,
        mesh=mesh,
        in_specs=(
            P("dp", None, None),
            P("dp", "sub", None),
            P("dp", "sub"),
            P("dp", "sub", None, None, None),
            P("dp", "sub", None),
            P("dp", "sub", None),
            P("sub", None, None),
        ),
        out_specs=P("dp", "sub", None),
        check_vma=False,
    )
```

```python
import functools

import jax
import jax.numpy as jnp
from jax import lax
from jax.experimental import pallas as pl
from jax.experimental.pallas import tpu as pltpu
from jax.sharding import PartitionSpec as P


DL = 512
LANES = 128
TILES = DL // LANES
PIECE = 32
PLAN_LANE = 96
score_scale = 192 ** (-0.5)
masked_score = -1e30


OWN_LIMIT = 24 << 20
PACK_LIMIT = 2 << 20
KERNEL_LIMIT = 14 << 20

VMEM = pl.BlockSpec(memory_space=pltpu.VMEM)
SMEM = pl.BlockSpec(memory_space=pltpu.SMEM)
HBM = pl.BlockSpec(memory_space=pltpu.HBM)


def lane_index(shape):
    return lax.broadcasted_iota(jnp.int32, shape, len(shape) - 1)


def pack_query_kernel(targets, plan_hbm, query_hbm, *refs):
    outs, (plan_ref, query_ref, sems) = refs[:-3], refs[-3:]
    plan_copy = pltpu.make_async_copy(plan_hbm, plan_ref, sems.at[0])
    query_copy = pltpu.make_async_copy(query_hbm, query_ref, sems.at[1])
    plan_copy.start()
    query_copy.start()
    me = lax.axis_index("dp")
    heads = query_ref.shape[1]
    half = heads // 2
    plan_copy.wait()
    query_copy.wait()
    for k, out in zip(targets, outs):
        r = plan_ref[me ^ k]
        for i in range(TILES):
            out[i * heads:(i + 1) * heads, :] = query_ref[r, :, i * LANES:(i + 1) * LANES]
        rotary = query_ref[r, :, DL:]
        out[TILES * heads:, :] = jnp.concatenate([rotary[:half], rotary[half:]], axis=1)


def unpack_query(packed_ref, heads):
    latent = jnp.concatenate(
        [packed_ref[i * heads:(i + 1) * heads, :] for i in range(TILES)], axis=1
    )
    tail = packed_ref[TILES * heads:, :]
    rotary = jnp.concatenate([tail[:, : LANES // 2], tail[:, LANES // 2:]], axis=0)
    return latent, rotary


def attend(latent, rotary, keys, length):
    width = keys.shape[1]
    scores = jnp.dot(latent, keys[:DL, :], preferred_element_type=jnp.float32)
    scores = scores + jnp.dot(rotary, keys[DL:, :], preferred_element_type=jnp.float32)
    scores = scores * score_scale
    scores = jnp.where(lane_index((1, width)) < length, scores, masked_score)
    largest = jnp.max(scores, axis=1, keepdims=True)
    exponent = jnp.exp(scores - largest)
    totals = jnp.sum(exponent, axis=1, keepdims=True)
    weights = exponent.astype(jnp.bfloat16)
    weighted = lax.dot_general(
        weights, keys[:DL, :], (((1,), (1,)), ((), ())), preferred_element_type=jnp.float32
    )
    return weighted / totals, largest + jnp.log(totals)


def put_lane(block, lane, column):
    return jnp.where(lane_index(block.shape) == lane, column, block)


def split_three(block):
    high = block.astype(jnp.bfloat16).astype(jnp.float32)
    rest = block - high
    middle = rest.astype(jnp.bfloat16).astype(jnp.float32)
    low = rest - middle
    return high + pltpu.roll(middle, PIECE, 1) + pltpu.roll(low, 2 * PIECE, 1)


def join_three(block):
    return block + pltpu.roll(block, LANES - PIECE, 1) + pltpu.roll(block, LANES - 2 * PIECE, 1)


def put_slot(stage, slot, rows, partial):
    heads = partial.shape[0]
    for i in range(TILES):
        stage[i, pl.ds(slot, heads, stride=rows), :] = partial[:, i * LANES:(i + 1) * LANES]


def write_messages(stage, side, rows, outs, part, other=None, taken=0):
    me = lax.axis_index("sub")
    for k, out in enumerate(outs):
        seat = me ^ k
        start = pl.multiple_of(seat * (part * rows), 8)
        for i in range(TILES):
            chunk = stage[i, pl.ds(start, part * rows), :]
            if taken:
                row = lax.broadcasted_iota(jnp.int32, chunk.shape, 0) % rows
                chunk = jnp.where(row < taken, other[i, pl.ds(start, part * rows), :], chunk)
            out[i * part * rows:(i + 1) * part * rows, :] = chunk.astype(jnp.bfloat16)
        side_start = pl.multiple_of(seat * part, 8)
        out[TILES * part * rows:, :] = side[pl.ds(side_start, part), :].astype(jnp.bfloat16)


def own_kernel(rows, plan_hbm, own_len_hbm, host_len_hbm, query_hbm, own_hbm, host_ref, cache_ref, stage, table_ref,
               plan_ref, own_len_ref, host_len_ref, query_ref, own_ref, first_sems, sems):
    me = lax.axis_index("dp")
    groups = host_ref.shape[0]
    firsts = []
    for i, (source, target) in enumerate((
        (query_hbm, query_ref), (own_hbm, own_ref), (plan_hbm, plan_ref),
        (own_len_hbm, own_len_ref), (host_len_hbm, host_len_ref),
    )):
        firsts.append(pltpu.make_async_copy(source, target, first_sems.at[i]))
        firsts[i].start()
    copies = []
    for k in range(groups):
        g = me ^ k
        copies.append(pltpu.make_async_copy(host_ref.at[g], cache_ref.at[g], sems.at[k]))
        copies[k].start()
    requests, heads, _ = query_ref.shape
    for copy in firsts:
        copy.wait()
    table = jnp.zeros((heads, LANES), jnp.float32)
    for r in range(requests):
        query = query_ref[r]
        partial, lse = attend(query[:, :DL], query[:, DL:], own_ref.at[r], own_len_ref[r])
        put_slot(stage, r, rows, partial)
        table = put_lane(table, r, lse)
    copies[0].wait()
    query = query_ref[plan_ref[me]]
    partial, lse = attend(query[:, :DL], query[:, DL:], cache_ref.at[me], host_len_ref[me])
    put_slot(stage, requests, rows, partial)
    table = put_lane(table, requests, lse)
    for p in range(groups):
        table = put_lane(table, PLAN_LANE + p, plan_ref[p].astype(jnp.float32))
    table_ref[...] = table
    for copy in copies[1:]:
        copy.wait()


def near_kernel(near, requests, rows, n_sub, host_len_ref, host_ref, own_stage, table_ref, *refs):
    packed, outs, (stage, side) = refs[: near - 1], refs[near - 1: near - 1 + n_sub], refs[near - 1 + n_sub:]
    me = lax.axis_index("dp")
    heads = side.shape[0]
    table = table_ref[...]
    lane = lane_index(table.shape)
    for k in range(1, near):
        g = me ^ k
        latent, rotary = unpack_query(packed[k - 1], heads)
        partial, lse = attend(latent, rotary, host_ref.at[g], host_len_ref[g])
        put_slot(stage, requests + k, rows, partial)
        table = put_lane(table, requests + k, lse)
    pieces = split_three(jnp.where(lane < PIECE, table, 0.0))
    side[...] = jnp.where(lane < PLAN_LANE, pieces, table)
    write_messages(stage, side, rows, outs, heads // n_sub, own_stage, requests + 1)


def far_kernel(near, rows, n_sub, host_len_ref, host_ref, *refs):
    groups = host_ref.shape[0]
    far = groups - near
    packed, outs, (stage, side) = refs[:far], refs[far: far + n_sub], refs[far + n_sub:]
    me = lax.axis_index("dp")
    heads = side.shape[0]
    table = jnp.zeros((heads, LANES), jnp.float32)
    if rows != far:
        stage[...] = jnp.zeros_like(stage)
    for j in range(far):
        g = me ^ (near + j)
        latent, rotary = unpack_query(packed[j], heads)
        partial, lse = attend(latent, rotary, host_ref.at[g], host_len_ref[g])
        put_slot(stage, j, rows, partial)
        table = put_lane(table, j, lse)
    side[...] = split_three(table)
    write_messages(stage, side, rows, outs, heads // n_sub)


def lift_kernel(near, requests, near_rows, far_rows, n_sub, groups, value_ref, *refs):
    near_in, far_in = refs[:n_sub], refs[n_sub: 2 * n_sub]
    out, own_out, own_side, lhs, lifted = refs[2 * n_sub:]
    me = lax.axis_index("dp")
    part = value_ref.shape[0]
    near_block, far_block = max(near_rows, 8), max(far_rows, 8)
    seats = n_sub * part
    for h in range(part):
        offset = 0
        for sources, rows, block in ((near_in, near_rows, near_block), (far_in, far_rows, far_block)):
            start = h * rows // block * block
            for source in sources:
                for i in range(TILES):
                    base = i * part * rows + start
                    lhs[h, offset: offset + block, i * LANES:(i + 1) * LANES] = source[base: base + block, :]
                offset += block
        result = jnp.dot(lhs[h], value_ref[h], preferred_element_type=jnp.float32)
        for s in range(n_sub):
            base = s * near_block
            lifted[pl.ds(s * part + h, near_block, stride=seats), :] = result[base: base + near_block]
            base = n_sub * near_block + s * far_block
            piece = result[base: base + far_block]
            skip = h * far_rows % far_block
            if skip:
                piece = pltpu.roll(piece, far_block - skip, 0)
            lifted[pl.ds(near_block * seats + s * part + h, far_block, stride=seats), :] = piece
    side_near = [ref[TILES * part * near_rows:, :].astype(jnp.float32) for ref in near_in]
    side_far = [ref[TILES * part * far_rows:, :].astype(jnp.float32) for ref in far_in]
    lane = lane_index((part, LANES))
    for k in range(groups):
        g = me ^ k
        row = requests + k if k < near else k - near
        first = (row if k < near else near_block + row) * seats
        out[g, :seats, :] = lifted[first: first + seats, :].astype(jnp.bfloat16)
        tile = jnp.zeros((part, LANES), jnp.float32)
        for s in range(n_sub):
            source = side_near[s] if k < near else side_far[s]
            moved = pltpu.roll(source, (s - row) % LANES, 1) if s != row else source
            tile = jnp.where((lane % PIECE == s) & (lane < 3 * PIECE), moved, tile)
        out[g, seats:, :] = tile.astype(jnp.bfloat16)
    own_out[...] = lifted[: requests * seats, :]
    for s in range(n_sub):
        own_side[s] = side_near[s]


def finish_kernel(requests, n_sub, groups, back_ref, own_ref, side_ref, out_ref):
    part = out_ref.shape[1]
    seats = n_sub * part
    lane = lane_index((part, LANES))
    sides = [side_ref[s] for s in range(n_sub)]
    joined = [join_three(side) for side in sides]
    help_lse, help_plan = [], []
    for p in range(groups):
        help_lse.append(join_three(back_ref[p, seats:, :].astype(jnp.float32)))
        plan = jnp.full((part, LANES), -1.0, jnp.float32)
        for s in range(n_sub):
            plan = put_lane(plan, s, sides[s][:, PLAN_LANE + p: PLAN_LANE + p + 1])
        help_plan.append(plan)
    peaks = []
    owns = []
    for r in range(requests):
        own = jnp.full((part, LANES), masked_score, jnp.float32)
        for s in range(n_sub):
            own = put_lane(own, s, joined[s][:, r: r + 1])
        peak = own
        for p in range(groups):
            peak = jnp.maximum(peak, jnp.where(help_plan[p] == r, help_lse[p], masked_score))
        peaks.append(jnp.max(peak, axis=1, keepdims=True))
        owns.append(own)
    for r in range(requests):
        own_weight = jnp.where(lane < n_sub, jnp.exp(owns[r] - peaks[r]), 0.0)
        total = own_weight
        summed = jnp.zeros((part, LANES), jnp.float32)
        for s in range(n_sub):
            first = (r * n_sub + s) * part
            summed = summed + own_weight[:, s: s + 1] * own_ref[first: first + part, :]
        for p in range(groups):
            chosen = help_plan[p] == r
            weight = jnp.exp(jnp.where(chosen, help_lse[p] - peaks[r], masked_score))
            total = total + weight
            for s in range(n_sub):
                value = back_ref[p, s * part:(s + 1) * part, :].astype(jnp.float32)
                summed = summed + weight[:, s: s + 1] * value
        total = jnp.sum(total, axis=1, keepdims=True)
        out_ref[r] = (summed / total).astype(jnp.bfloat16)


def exchange(array, axis, k):
    size = lax.axis_size(axis)
    return lax.ppermute(array, axis, [(i, i ^ k) for i in range(size)])


def call(kernel, outs, in_specs, scratch=(), limit=None, cost=None):
    def run(*args):
        return pl.pallas_call(
            kernel,
            out_shape=outs,
            in_specs=in_specs,
            out_specs=jax.tree.map(lambda _: VMEM, outs),
            scratch_shapes=list(scratch),
            compiler_params=pltpu.CompilerParams(vmem_limit_bytes=limit),
            cost_estimate=cost,
        )(*args)

    return run


def in_hbm(array):
    return pltpu.with_memory_space_constraint(array, pltpu.HBM)


def near_count(groups):
    return min(4, groups)


def local(queries, own_cache, own_len, host_cache, host_len, page_plan, value_up):
    groups, n_sub = lax.axis_size("dp"), lax.axis_size("sub")
    requests, heads, width = queries.shape
    part = heads // n_sub
    slot_tokens = host_cache.shape[3]
    near = near_count(groups)
    far = groups - near
    near_rows = requests + near
    far_rows = far if far in (1, 2, 4) else -(-far // 8) * 8
    plan = page_plan.reshape(groups)
    lengths = host_len.reshape(groups)
    own_lengths = own_len.reshape(requests)
    own_keys = jnp.swapaxes(own_cache, 1, 2)
    host_keys = jnp.swapaxes(host_cache.reshape(groups, slot_tokens, width), 1, 2)

    targets = list(range(1, groups))
    packed = jax.ShapeDtypeStruct((heads * width // LANES, LANES), jnp.bfloat16)
    outgoing = call(
        functools.partial(pack_query_kernel, targets), [packed] * len(targets), [HBM, HBM],
        [pltpu.SMEM(plan.shape, plan.dtype), pltpu.VMEM(queries.shape, queries.dtype), pltpu.SemaphoreType.DMA((2,))],
        limit=PACK_LIMIT,
    )(in_hbm(plan), in_hbm(queries))
    order = list(range(near, groups)) + list(range(1, near))
    received = {k: exchange(outgoing[k - 1], "dp", k) for k in order}

    def message(rows):
        return jax.ShapeDtypeStruct((TILES * part * rows + part, LANES), jnp.bfloat16)

    def stage_shape(rows):
        return (TILES, heads * rows, LANES)

    def stages(rows):
        return [pltpu.VMEM(stage_shape(rows), jnp.float32), pltpu.VMEM((heads, LANES), jnp.float32)]

    def cost(slots):
        return pl.CostEstimate(
            flops=2 * slots * heads * slot_tokens * (width + DL),
            bytes_accessed=2 * slots * slot_tokens * width,
            transcendentals=slots * heads * slot_tokens,
        )

    cache, own_stage, table = call(
        functools.partial(own_kernel, near_rows),
        [
            jax.ShapeDtypeStruct(host_keys.shape, host_keys.dtype),
            jax.ShapeDtypeStruct(stage_shape(near_rows), jnp.float32),
            jax.ShapeDtypeStruct((heads, LANES), jnp.float32),
        ],
        [HBM] * 6,
        [
            pltpu.SMEM(plan.shape, plan.dtype),
            pltpu.SMEM(own_lengths.shape, own_lengths.dtype),
            pltpu.SMEM(lengths.shape, lengths.dtype),
            pltpu.VMEM(queries.shape, queries.dtype),
            pltpu.VMEM(own_keys.shape, own_keys.dtype),
            pltpu.SemaphoreType.DMA((5,)),
            pltpu.SemaphoreType.DMA((groups,)),
        ],
        limit=OWN_LIMIT,
        cost=cost(groups),
    )(*[in_hbm(x) for x in (plan, own_lengths, lengths, queries, own_keys, host_keys)])
    near_out = call(
        functools.partial(near_kernel, near, requests, near_rows, n_sub),
        [message(near_rows)] * n_sub,
        [SMEM] + [VMEM] * (3 + near - 1),
        stages(near_rows),
        limit=KERNEL_LIMIT,
        cost=cost(near - 1),
    )(lengths, cache, own_stage, table, *[received[k] for k in range(1, near)])
    far_out = call(
        functools.partial(far_kernel, near, far_rows, n_sub),
        [message(far_rows)] * n_sub,
        [SMEM] + [VMEM] * (1 + far),
        stages(far_rows),
        limit=KERNEL_LIMIT,
        cost=cost(far),
    )(lengths, cache, *[received[k] for k in range(near, groups)])
    sub_order = [k for k in range(2, n_sub)] + [1]
    near_in, far_in = {0: near_out[0]}, {0: far_out[0]}
    for k in sub_order:
        near_in[k] = exchange(near_out[k], "sub", k)
    for k in sub_order:
        far_in[k] = exchange(far_out[k], "sub", k)

    near_block, far_block = max(near_rows, 8), max(far_rows, 8)
    seats = n_sub * part
    back, own, side = call(
        functools.partial(lift_kernel, near, requests, near_rows, far_rows, n_sub, groups),
        [
            jax.ShapeDtypeStruct((groups, seats + part, LANES), jnp.bfloat16),
            jax.ShapeDtypeStruct((requests * seats, LANES), jnp.float32),
            jax.ShapeDtypeStruct((n_sub, part, LANES), jnp.float32),
        ],
        [VMEM] * (1 + 2 * n_sub),
        [
            pltpu.VMEM((part, n_sub * (near_block + far_block), DL), jnp.bfloat16),
            pltpu.VMEM(((near_block + far_block) * seats, LANES), jnp.float32),
        ],
        limit=12 << 20,
    )(value_up, *[near_in[k] for k in range(n_sub)], *[far_in[k] for k in range(n_sub)])
    back = lax.all_to_all(back, "dp", split_axis=0, concat_axis=0, tiled=True)
    return call(
        functools.partial(finish_kernel, requests, n_sub, groups),
        jax.ShapeDtypeStruct((requests, part, LANES), jnp.bfloat16),
        [VMEM] * 3,
        limit=4 << 20,
    )(back, own, side)


def solution(mesh):
    return jax.shard_map(
        local,
        mesh=mesh,
        in_specs=(
            P("dp", None, None),
            P("dp", "sub", None),
            P("dp", "sub"),
            P("dp", "sub", None, None, None),
            P("dp", "sub", None),
            P("dp", "sub", None),
            P("sub", None, None),
        ),
        out_specs=P("dp", "sub", None),
        check_vma=False,
    )
```

```python
import functools

import jax
import jax.numpy as jnp
from jax import lax
from jax.experimental import pallas as pl
from jax.experimental.pallas import tpu as pltpu
from jax.sharding import PartitionSpec as P


DL = 512
LANES = 128
TILES = DL // LANES
PIECE = 32
PLAN_LANE = 96
score_scale = 192 ** (-0.5)
masked_score = -1e30


OWN_LIMIT = 24 << 20
PACK_LIMIT = 2 << 20
KERNEL_LIMIT = 14 << 20

VMEM = pl.BlockSpec(memory_space=pltpu.VMEM)
SMEM = pl.BlockSpec(memory_space=pltpu.SMEM)
HBM = pl.BlockSpec(memory_space=pltpu.HBM)


def lane_index(shape):
    return lax.broadcasted_iota(jnp.int32, shape, len(shape) - 1)


def pack_query_kernel(targets, plan_hbm, query_hbm, *refs):
    outs, (plan_ref, query_ref, sems) = refs[:-3], refs[-3:]
    plan_copy = pltpu.make_async_copy(plan_hbm, plan_ref, sems.at[0])
    query_copy = pltpu.make_async_copy(query_hbm, query_ref, sems.at[1])
    plan_copy.start()
    query_copy.start()
    me = lax.axis_index("dp")
    heads = query_ref.shape[1]
    half = heads // 2
    plan_copy.wait()
    query_copy.wait()
    for k, out in zip(targets, outs):
        r = plan_ref[me ^ k]
        for i in range(TILES):
            out[i * heads:(i + 1) * heads, :] = query_ref[r, :, i * LANES:(i + 1) * LANES]
        rotary = query_ref[r, :, DL:]
        out[TILES * heads:, :] = jnp.concatenate([rotary[:half], rotary[half:]], axis=1)


def unpack_query(packed_ref, heads):
    latent = jnp.concatenate(
        [packed_ref[i * heads:(i + 1) * heads, :] for i in range(TILES)], axis=1
    )
    tail = packed_ref[TILES * heads:, :]
    rotary = jnp.concatenate([tail[:, : LANES // 2], tail[:, LANES // 2:]], axis=0)
    return latent, rotary


def attend(latent, rotary, keys, length):
    width = keys.shape[1]
    scores = jnp.dot(latent, keys[:DL, :], preferred_element_type=jnp.float32)
    scores = scores + jnp.dot(rotary, keys[DL:, :], preferred_element_type=jnp.float32)
    scores = scores * score_scale
    scores = jnp.where(lane_index((1, width)) < length, scores, masked_score)
    largest = jnp.max(scores, axis=1, keepdims=True)
    exponent = jnp.exp(scores - largest)
    totals = jnp.sum(exponent, axis=1, keepdims=True)
    weights = exponent.astype(jnp.bfloat16)
    weighted = lax.dot_general(
        weights, keys[:DL, :], (((1,), (1,)), ((), ())), preferred_element_type=jnp.float32
    )
    return weighted / totals, largest + jnp.log(totals)


def put_lane(block, lane, column):
    return jnp.where(lane_index(block.shape) == lane, column, block)


def split_three(block):
    high = block.astype(jnp.bfloat16).astype(jnp.float32)
    rest = block - high
    middle = rest.astype(jnp.bfloat16).astype(jnp.float32)
    low = rest - middle
    return high + pltpu.roll(middle, PIECE, 1) + pltpu.roll(low, 2 * PIECE, 1)


def join_three(block):
    return block + pltpu.roll(block, LANES - PIECE, 1) + pltpu.roll(block, LANES - 2 * PIECE, 1)


def put_slot(stage, slot, rows, partial):
    heads = partial.shape[0]
    for i in range(TILES):
        stage[i, pl.ds(slot, heads, stride=rows), :] = partial[:, i * LANES:(i + 1) * LANES]


def write_messages(stage, side, rows, outs, part):
    me = lax.axis_index("sub")
    for k, out in enumerate(outs):
        seat = me ^ k
        start = pl.multiple_of(seat * (part * rows), 8)
        for i in range(TILES):
            chunk = stage[i, pl.ds(start, part * rows), :]
            out[i * part * rows:(i + 1) * part * rows, :] = chunk.astype(jnp.bfloat16)
        side_start = pl.multiple_of(seat * part, 8)
        out[TILES * part * rows:, :] = side[pl.ds(side_start, part), :].astype(jnp.bfloat16)


def own_kernel(rows, n_sub, plan_hbm, own_len_hbm, query_hbm, own_hbm, host_ref, cache_ref, self_ref, *refs):
    outs, (plan_ref, own_len_ref, query_ref, own_ref, stage, side, first_sems, sems) = refs[:n_sub], refs[n_sub:]
    me = lax.axis_index("dp")
    groups = host_ref.shape[0]
    firsts = []
    for i, (source, target) in enumerate((
        (query_hbm, query_ref), (own_hbm, own_ref), (plan_hbm, plan_ref),
        (own_len_hbm, own_len_ref),
    )):
        firsts.append(pltpu.make_async_copy(source, target, first_sems.at[i]))
        firsts[i].start()
    copies = []
    for k in range(groups):
        g = me ^ k
        copies.append(pltpu.make_async_copy(host_ref.at[g], cache_ref.at[g], sems.at[k]))
        copies[k].start()
    requests, heads, _ = query_ref.shape
    for copy in firsts:
        copy.wait()
    table = jnp.zeros((heads, LANES), jnp.float32)
    for r in range(requests):
        query = query_ref[r]
        partial, lse = attend(query[:, :DL], query[:, DL:], own_ref.at[r], own_len_ref[r])
        put_slot(stage, r, rows, partial)
        table = put_lane(table, r, lse)
    self_ref[...] = query_ref[plan_ref[me]]
    table = split_three(table)
    for p in range(groups):
        table = put_lane(table, PLAN_LANE + p, plan_ref[p].astype(jnp.float32))
    side[...] = table
    write_messages(stage, side, rows, outs, heads // n_sub)
    for copy in copies:
        copy.wait()


def near_kernel(near, rows, n_sub, host_len_ref, host_ref, self_ref, *refs):
    packed, outs, (stage, side) = refs[: near - 1], refs[near - 1: near - 1 + n_sub], refs[near - 1 + n_sub:]
    me = lax.axis_index("dp")
    heads = side.shape[0]
    table = jnp.zeros((heads, LANES), jnp.float32)
    for k in range(near):
        g = me ^ k
        if k == 0:
            latent, rotary = self_ref[:, :DL], self_ref[:, DL:]
        else:
            latent, rotary = unpack_query(packed[k - 1], heads)
        partial, lse = attend(latent, rotary, host_ref.at[g], host_len_ref[g])
        put_slot(stage, k, rows, partial)
        table = put_lane(table, k, lse)
    side[...] = split_three(table)
    write_messages(stage, side, rows, outs, heads // n_sub)


def far_kernel(near, rows, n_sub, host_len_ref, host_ref, *refs):
    groups = host_ref.shape[0]
    far = groups - near
    packed, outs, (stage, side) = refs[:far], refs[far: far + n_sub], refs[far + n_sub:]
    me = lax.axis_index("dp")
    heads = side.shape[0]
    table = jnp.zeros((heads, LANES), jnp.float32)
    if rows != far:
        stage[...] = jnp.zeros_like(stage)
    for j in range(far):
        g = me ^ (near + j)
        latent, rotary = unpack_query(packed[j], heads)
        partial, lse = attend(latent, rotary, host_ref.at[g], host_len_ref[g])
        put_slot(stage, j, rows, partial)
        table = put_lane(table, j, lse)
    side[...] = split_three(table)
    write_messages(stage, side, rows, outs, heads // n_sub)


def lift_kernel(near, chunk_rows, n_sub, groups, value_ref, *refs):
    chunks = len(chunk_rows)
    sources = [refs[c * n_sub:(c + 1) * n_sub] for c in range(chunks)]
    out, own_out, own_side, lhs, lifted = refs[chunks * n_sub:]
    me = lax.axis_index("dp")
    part = value_ref.shape[0]
    seats = n_sub * part
    blocks = [max(rows, 8) for rows in chunk_rows]
    for h in range(part):
        offset = 0
        for refs_of, rows, block in zip(sources, chunk_rows, blocks):
            start = h * rows // block * block
            for source in refs_of:
                for i in range(TILES):
                    base = i * part * rows + start
                    lhs[h, offset: offset + block, i * LANES:(i + 1) * LANES] = source[base: base + block, :]
                offset += block
        result = jnp.dot(lhs[h], value_ref[h], preferred_element_type=jnp.float32)
        offset, slot = 0, 0
        for rows, block in zip(chunk_rows, blocks):
            skip = h * rows % block
            for s in range(n_sub):
                piece = result[offset: offset + block]
                if skip:
                    piece = pltpu.roll(piece, block - skip, 0)
                lifted[pl.ds(slot * seats + s * part + h, block, stride=seats), :] = piece
                offset += block
            slot += block
    sides = [
        [ref[TILES * part * rows:, :].astype(jnp.float32) for ref in refs_of]
        for refs_of, rows in zip(sources, chunk_rows)
    ]
    lane = lane_index((part, LANES))
    for k in range(groups):
        chunk, row = (1, k) if k < near else (2, k - near)
        first = (sum(blocks[:chunk]) + row) * seats
        out[me ^ k, :seats, :] = lifted[first: first + seats, :].astype(jnp.bfloat16)
        tile = jnp.zeros((part, LANES), jnp.float32)
        for s in range(n_sub):
            source = sides[chunk][s]
            moved = pltpu.roll(source, (s - row) % LANES, 1) if s != row else source
            tile = jnp.where((lane % PIECE == s) & (lane < 3 * PIECE), moved, tile)
        out[me ^ k, seats:, :] = tile.astype(jnp.bfloat16)
    own_out[...] = lifted[: own_out.shape[0], :]
    for s in range(n_sub):
        own_side[s] = sides[0][s]


def finish_kernel(requests, n_sub, groups, back_ref, own_ref, side_ref, out_ref):
    part = out_ref.shape[1]
    seats = n_sub * part
    lane = lane_index((part, LANES))
    sides = [side_ref[s] for s in range(n_sub)]
    joined = [join_three(side) for side in sides]
    help_lse, help_plan = [], []
    for p in range(groups):
        help_lse.append(join_three(back_ref[p, seats:, :].astype(jnp.float32)))
        plan = jnp.full((part, LANES), -1.0, jnp.float32)
        for s in range(n_sub):
            plan = put_lane(plan, s, sides[s][:, PLAN_LANE + p: PLAN_LANE + p + 1])
        help_plan.append(plan)
    peaks = []
    owns = []
    for r in range(requests):
        own = jnp.full((part, LANES), masked_score, jnp.float32)
        for s in range(n_sub):
            own = put_lane(own, s, joined[s][:, r: r + 1])
        peak = own
        for p in range(groups):
            peak = jnp.maximum(peak, jnp.where(help_plan[p] == r, help_lse[p], masked_score))
        peaks.append(jnp.max(peak, axis=1, keepdims=True))
        owns.append(own)
    for r in range(requests):
        own_weight = jnp.where(lane < n_sub, jnp.exp(owns[r] - peaks[r]), 0.0)
        total = own_weight
        summed = jnp.zeros((part, LANES), jnp.float32)
        for s in range(n_sub):
            first = (r * n_sub + s) * part
            summed = summed + own_weight[:, s: s + 1] * own_ref[first: first + part, :]
        for p in range(groups):
            chosen = help_plan[p] == r
            weight = jnp.exp(jnp.where(chosen, help_lse[p] - peaks[r], masked_score))
            total = total + weight
            for s in range(n_sub):
                value = back_ref[p, s * part:(s + 1) * part, :].astype(jnp.float32)
                summed = summed + weight[:, s: s + 1] * value
        total = jnp.sum(total, axis=1, keepdims=True)
        out_ref[r] = (summed / total).astype(jnp.bfloat16)


def exchange(array, axis, k):
    size = lax.axis_size(axis)
    return lax.ppermute(array, axis, [(i, i ^ k) for i in range(size)])


def call(kernel, outs, in_specs, scratch=(), limit=None, cost=None):
    def run(*args):
        return pl.pallas_call(
            kernel,
            out_shape=outs,
            in_specs=in_specs,
            out_specs=jax.tree.map(lambda _: VMEM, outs),
            scratch_shapes=list(scratch),
            compiler_params=pltpu.CompilerParams(vmem_limit_bytes=limit),
            cost_estimate=cost,
        )(*args)

    return run


def in_hbm(array):
    return pltpu.with_memory_space_constraint(array, pltpu.HBM)


def padded_rows(count):
    return count if count in (1, 2, 4) else -(-count // 8) * 8


def near_count(groups):
    return min(4, groups)


def local(queries, own_cache, own_len, host_cache, host_len, page_plan, value_up):
    groups, n_sub = lax.axis_size("dp"), lax.axis_size("sub")
    requests, heads, width = queries.shape
    part = heads // n_sub
    slot_tokens = host_cache.shape[3]
    near = near_count(groups)
    far = groups - near
    own_rows, near_rows, far_rows = padded_rows(requests), padded_rows(near), padded_rows(far)
    plan = page_plan.reshape(groups)
    lengths = host_len.reshape(groups)
    own_lengths = own_len.reshape(requests)
    own_keys = jnp.swapaxes(own_cache, 1, 2)
    host_keys = jnp.swapaxes(host_cache.reshape(groups, slot_tokens, width), 1, 2)

    targets = list(range(1, groups))
    packed = jax.ShapeDtypeStruct((heads * width // LANES, LANES), jnp.bfloat16)
    outgoing = call(
        functools.partial(pack_query_kernel, targets), [packed] * len(targets), [HBM, HBM],
        [pltpu.SMEM(plan.shape, plan.dtype), pltpu.VMEM(queries.shape, queries.dtype), pltpu.SemaphoreType.DMA((2,))],
        limit=PACK_LIMIT,
    )(in_hbm(plan), in_hbm(queries))
    order = list(range(near, groups)) + list(range(1, near))
    received = {k: exchange(outgoing[k - 1], "dp", k) for k in order}

    def message(rows):
        return jax.ShapeDtypeStruct((TILES * part * rows + part, LANES), jnp.bfloat16)

    def stage_shape(rows):
        return (TILES, heads * rows, LANES)

    def stages(rows):
        return [pltpu.VMEM(stage_shape(rows), jnp.float32), pltpu.VMEM((heads, LANES), jnp.float32)]

    def cost(slots):
        return pl.CostEstimate(
            flops=2 * slots * heads * slot_tokens * (width + DL),
            bytes_accessed=2 * slots * slot_tokens * width,
            transcendentals=slots * heads * slot_tokens,
        )

    cache, self_query, *own_out = call(
        functools.partial(own_kernel, own_rows, n_sub),
        [
            jax.ShapeDtypeStruct(host_keys.shape, host_keys.dtype),
            jax.ShapeDtypeStruct((heads, width), queries.dtype),
        ] + [message(own_rows)] * n_sub,
        [HBM] * 5,
        [
            pltpu.SMEM(plan.shape, plan.dtype),
            pltpu.SMEM(own_lengths.shape, own_lengths.dtype),
            pltpu.VMEM(queries.shape, queries.dtype),
            pltpu.VMEM(own_keys.shape, own_keys.dtype),
        ] + stages(own_rows) + [
            pltpu.SemaphoreType.DMA((4,)),
            pltpu.SemaphoreType.DMA((groups,)),
        ],
        limit=OWN_LIMIT,
        cost=cost(groups),
    )(*[in_hbm(x) for x in (plan, own_lengths, queries, own_keys, host_keys)])
    near_out = call(
        functools.partial(near_kernel, near, near_rows, n_sub),
        [message(near_rows)] * n_sub,
        [SMEM] + [VMEM] * (2 + near - 1),
        stages(near_rows),
        limit=KERNEL_LIMIT,
        cost=cost(near),
    )(lengths, cache, self_query, *[received[k] for k in range(1, near)])
    far_out = call(
        functools.partial(far_kernel, near, far_rows, n_sub),
        [message(far_rows)] * n_sub,
        [SMEM] + [VMEM] * (1 + far),
        stages(far_rows),
        limit=KERNEL_LIMIT,
        cost=cost(far),
    )(lengths, cache, *[received[k] for k in range(near, groups)])
    sub_order = [k for k in range(2, n_sub)] + [1]
    arrived = []
    for messages in (own_out, near_out, far_out):
        moved = {k: exchange(messages[k], "sub", k) for k in sub_order}
        arrived += [messages[0]] + [moved[k] for k in range(1, n_sub)]

    chunk_rows = (own_rows, near_rows, far_rows)
    slots = sum(max(rows, 8) for rows in chunk_rows)
    seats = n_sub * part
    back, own, side = call(
        functools.partial(lift_kernel, near, chunk_rows, n_sub, groups),
        [
            jax.ShapeDtypeStruct((groups, seats + part, LANES), jnp.bfloat16),
            jax.ShapeDtypeStruct((requests * seats, LANES), jnp.float32),
            jax.ShapeDtypeStruct((n_sub, part, LANES), jnp.float32),
        ],
        [VMEM] * (1 + 3 * n_sub),
        [
            pltpu.VMEM((part, n_sub * slots, DL), jnp.bfloat16),
            pltpu.VMEM((slots * seats, LANES), jnp.float32),
        ],
        limit=12 << 20,
    )(value_up, *arrived)
    back = lax.all_to_all(back, "dp", split_axis=0, concat_axis=0, tiled=True)
    return call(
        functools.partial(finish_kernel, requests, n_sub, groups),
        jax.ShapeDtypeStruct((requests, part, LANES), jnp.bfloat16),
        [VMEM] * 3,
        limit=4 << 20,
    )(back, own, side)


def solution(mesh):
    return jax.shard_map(
        local,
        mesh=mesh,
        in_specs=(
            P("dp", None, None),
            P("dp", "sub", None),
            P("dp", "sub"),
            P("dp", "sub", None, None, None),
            P("dp", "sub", None),
            P("dp", "sub", None),
            P("sub", None, None),
        ),
        out_specs=P("dp", "sub", None),
        check_vma=False,
    )
```

```python
import functools

import jax
import jax.numpy as jnp
from jax import lax
from jax.experimental import pallas as pl
from jax.experimental.pallas import tpu as pltpu
from jax.sharding import PartitionSpec as P


DL = 512
LANES = 128
TILES = DL // LANES
PIECE = 32
PLAN_LANE = 96
score_scale = 192 ** (-0.5)
masked_score = -1e30


OWN_LIMIT = 24 << 20
PACK_LIMIT = 2 << 20
KERNEL_LIMIT = 14 << 20

VMEM = pl.BlockSpec(memory_space=pltpu.VMEM)
SMEM = pl.BlockSpec(memory_space=pltpu.SMEM)
HBM = pl.BlockSpec(memory_space=pltpu.HBM)


def lane_index(shape):
    return lax.broadcasted_iota(jnp.int32, shape, len(shape) - 1)


def pack_query_kernel(targets, plan_hbm, query_hbm, *refs):
    outs, (plan_ref, query_ref, sems) = refs[:-3], refs[-3:]
    plan_copy = pltpu.make_async_copy(plan_hbm, plan_ref, sems.at[0])
    query_copy = pltpu.make_async_copy(query_hbm, query_ref, sems.at[1])
    plan_copy.start()
    query_copy.start()
    me = lax.axis_index("dp")
    heads = query_ref.shape[1]
    half = heads // 2
    plan_copy.wait()
    query_copy.wait()
    for k, out in zip(targets, outs):
        r = plan_ref[me ^ k]
        for i in range(TILES):
            out[i * heads:(i + 1) * heads, :] = query_ref[r, :, i * LANES:(i + 1) * LANES]
        rotary = query_ref[r, :, DL:]
        out[TILES * heads:, :] = jnp.concatenate([rotary[:half], rotary[half:]], axis=1)


def unpack_query(packed_ref, heads):
    latent = jnp.concatenate(
        [packed_ref[i * heads:(i + 1) * heads, :] for i in range(TILES)], axis=1
    )
    tail = packed_ref[TILES * heads:, :]
    rotary = jnp.concatenate([tail[:, : LANES // 2], tail[:, LANES // 2:]], axis=0)
    return latent, rotary


def attend(latent, rotary, keys, length):
    width = keys.shape[1]
    scores = jnp.dot(latent, keys[:DL, :], preferred_element_type=jnp.float32)
    scores = scores + jnp.dot(rotary, keys[DL:, :], preferred_element_type=jnp.float32)
    scores = scores * score_scale
    scores = jnp.where(lane_index((1, width)) < length, scores, masked_score)
    largest = jnp.max(scores, axis=1, keepdims=True)
    exponent = jnp.exp(scores - largest)
    totals = jnp.sum(exponent, axis=1, keepdims=True)
    weights = exponent.astype(jnp.bfloat16)
    weighted = lax.dot_general(
        weights, keys[:DL, :], (((1,), (1,)), ((), ())), preferred_element_type=jnp.float32
    )
    return weighted / totals, largest + jnp.log(totals)


def put_lane(block, lane, column):
    return jnp.where(lane_index(block.shape) == lane, column, block)


def split_three(block):
    high = block.astype(jnp.bfloat16).astype(jnp.float32)
    rest = block - high
    middle = rest.astype(jnp.bfloat16).astype(jnp.float32)
    low = rest - middle
    return high + pltpu.roll(middle, PIECE, 1) + pltpu.roll(low, 2 * PIECE, 1)


def join_three(block):
    return block + pltpu.roll(block, LANES - PIECE, 1) + pltpu.roll(block, LANES - 2 * PIECE, 1)


def put_slot(stage, slot, rows, partial):
    heads = partial.shape[0]
    for i in range(TILES):
        stage[i, pl.ds(slot, heads, stride=rows), :] = partial[:, i * LANES:(i + 1) * LANES]


def write_messages(stage, side, rows, outs, part, other=None, taken=0):
    me = lax.axis_index("sub")
    for k, out in enumerate(outs):
        seat = me ^ k
        start = pl.multiple_of(seat * (part * rows), 8)
        for i in range(TILES):
            chunk = stage[i, pl.ds(start, part * rows), :]
            if taken:
                row = lax.broadcasted_iota(jnp.int32, chunk.shape, 0) % rows
                chunk = jnp.where(row < taken, other[i, pl.ds(start, part * rows), :], chunk)
            out[i * part * rows:(i + 1) * part * rows, :] = chunk.astype(jnp.bfloat16)
        side_start = pl.multiple_of(seat * part, 8)
        out[TILES * part * rows:, :] = side[pl.ds(side_start, part), :].astype(jnp.bfloat16)


def own_kernel(rows, plan_hbm, own_len_hbm, host_len_hbm, query_hbm, own_hbm, host_ref, cache_ref, stage, table_ref,
               plan_ref, own_len_ref, host_len_ref, query_ref, own_ref, first_sems, sems):
    me = lax.axis_index("dp")
    groups = host_ref.shape[0]
    firsts = []
    for i, (source, target) in enumerate((
        (query_hbm, query_ref), (own_hbm, own_ref), (plan_hbm, plan_ref),
        (own_len_hbm, own_len_ref), (host_len_hbm, host_len_ref),
    )):
        firsts.append(pltpu.make_async_copy(source, target, first_sems.at[i]))
        firsts[i].start()
    copies = []
    for k in range(groups):
        g = me ^ k
        copies.append(pltpu.make_async_copy(host_ref.at[g], cache_ref.at[g], sems.at[k]))
        copies[k].start()
    requests, heads, _ = query_ref.shape
    for copy in firsts:
        copy.wait()
    table = jnp.zeros((heads, LANES), jnp.float32)
    for r in range(requests):
        query = query_ref[r]
        partial, lse = attend(query[:, :DL], query[:, DL:], own_ref.at[r], own_len_ref[r])
        put_slot(stage, r, rows, partial)
        table = put_lane(table, r, lse)
    copies[0].wait()
    query = query_ref[plan_ref[me]]
    partial, lse = attend(query[:, :DL], query[:, DL:], cache_ref.at[me], host_len_ref[me])
    put_slot(stage, requests, rows, partial)
    table = put_lane(table, requests, lse)
    for p in range(groups):
        table = put_lane(table, PLAN_LANE + p, plan_ref[p].astype(jnp.float32))
    table_ref[...] = table
    for copy in copies[1:]:
        copy.wait()


def near_kernel(near, requests, rows, n_sub, host_len_ref, host_ref, own_stage, table_ref, *refs):
    packed, outs, (stage, side) = refs[: near - 1], refs[near - 1: near - 1 + n_sub], refs[near - 1 + n_sub:]
    me = lax.axis_index("dp")
    heads = side.shape[0]
    table = table_ref[...]
    lane = lane_index(table.shape)
    for k in range(1, near):
        g = me ^ k
        latent, rotary = unpack_query(packed[k - 1], heads)
        partial, lse = attend(latent, rotary, host_ref.at[g], host_len_ref[g])
        put_slot(stage, requests + k, rows, partial)
        table = put_lane(table, requests + k, lse)
    pieces = split_three(jnp.where(lane < PIECE, table, 0.0))
    side[...] = jnp.where(lane < PLAN_LANE, pieces, table)
    write_messages(stage, side, rows, outs, heads // n_sub, own_stage, requests + 1)


def far_kernel(near, rows, n_sub, host_len_ref, host_ref, *refs):
    groups = host_ref.shape[0]
    far = groups - near
    packed, outs, (stage, side) = refs[:far], refs[far: far + n_sub], refs[far + n_sub:]
    me = lax.axis_index("dp")
    heads = side.shape[0]
    table = jnp.zeros((heads, LANES), jnp.float32)
    if rows != far:
        stage[...] = jnp.zeros_like(stage)
    for j in range(far):
        g = me ^ (near + j)
        latent, rotary = unpack_query(packed[j], heads)
        partial, lse = attend(latent, rotary, host_ref.at[g], host_len_ref[g])
        put_slot(stage, j, rows, partial)
        table = put_lane(table, j, lse)
    side[...] = split_three(table)
    write_messages(stage, side, rows, outs, heads // n_sub)


def lift_kernel(near, requests, near_rows, far_rows, n_sub, groups, value_ref, *refs):
    near_in, far_in = refs[:n_sub], refs[n_sub: 2 * n_sub]
    out, own_out, own_side, lhs, lifted = refs[2 * n_sub:]
    me = lax.axis_index("dp")
    part = value_ref.shape[0]
    near_block, far_block = max(near_rows, 8), max(far_rows, 8)
    seats = n_sub * part
    for h in range(part):
        offset = 0
        for sources, rows, block in ((near_in, near_rows, near_block), (far_in, far_rows, far_block)):
            start = h * rows // block * block
            for source in sources:
                for i in range(TILES):
                    base = i * part * rows + start
                    lhs[h, offset: offset + block, i * LANES:(i + 1) * LANES] = source[base: base + block, :]
                offset += block
        result = jnp.dot(lhs[h], value_ref[h], preferred_element_type=jnp.float32)
        for s in range(n_sub):
            base = s * near_block
            lifted[pl.ds(s * part + h, near_block, stride=seats), :] = result[base: base + near_block]
            base = n_sub * near_block + s * far_block
            piece = result[base: base + far_block]
            skip = h * far_rows % far_block
            if skip:
                piece = pltpu.roll(piece, far_block - skip, 0)
            lifted[pl.ds(near_block * seats + s * part + h, far_block, stride=seats), :] = piece
    side_near = [ref[TILES * part * near_rows:, :].astype(jnp.float32) for ref in near_in]
    side_far = [ref[TILES * part * far_rows:, :].astype(jnp.float32) for ref in far_in]
    lane = lane_index((part, LANES))
    for k in range(groups):
        g = me ^ k
        row = requests + k if k < near else k - near
        first = (row if k < near else near_block + row) * seats
        out[g, :seats, :] = lifted[first: first + seats, :].astype(jnp.bfloat16)
        tile = jnp.zeros((part, LANES), jnp.float32)
        for s in range(n_sub):
            source = side_near[s] if k < near else side_far[s]
            moved = pltpu.roll(source, (s - row) % LANES, 1) if s != row else source
            tile = jnp.where((lane % PIECE == s) & (lane < 3 * PIECE), moved, tile)
        out[g, seats:, :] = tile.astype(jnp.bfloat16)
    own_out[...] = lifted[: requests * seats, :]
    for s in range(n_sub):
        own_side[s] = side_near[s]


def finish_kernel(requests, n_sub, groups, back_ref, own_ref, side_ref, out_ref):
    part = out_ref.shape[1]
    seats = n_sub * part
    lane = lane_index((part, LANES))
    sides = [side_ref[s] for s in range(n_sub)]
    joined = [join_three(side) for side in sides]
    help_lse, help_plan = [], []
    for p in range(groups):
        help_lse.append(join_three(back_ref[p, seats:, :].astype(jnp.float32)))
        plan = jnp.full((part, LANES), -1.0, jnp.float32)
        for s in range(n_sub):
            plan = put_lane(plan, s, sides[s][:, PLAN_LANE + p: PLAN_LANE + p + 1])
        help_plan.append(plan)
    peaks = []
    owns = []
    for r in range(requests):
        own = jnp.full((part, LANES), masked_score, jnp.float32)
        for s in range(n_sub):
            own = put_lane(own, s, joined[s][:, r: r + 1])
        peak = own
        for p in range(groups):
            peak = jnp.maximum(peak, jnp.where(help_plan[p] == r, help_lse[p], masked_score))
        peaks.append(jnp.max(peak, axis=1, keepdims=True))
        owns.append(own)
    for r in range(requests):
        own_weight = jnp.where(lane < n_sub, jnp.exp(owns[r] - peaks[r]), 0.0)
        total = own_weight
        summed = jnp.zeros((part, LANES), jnp.float32)
        for s in range(n_sub):
            first = (r * n_sub + s) * part
            summed = summed + own_weight[:, s: s + 1] * own_ref[first: first + part, :]
        for p in range(groups):
            chosen = help_plan[p] == r
            weight = jnp.exp(jnp.where(chosen, help_lse[p] - peaks[r], masked_score))
            total = total + weight
            for s in range(n_sub):
                value = back_ref[p, s * part:(s + 1) * part, :].astype(jnp.float32)
                summed = summed + weight[:, s: s + 1] * value
        total = jnp.sum(total, axis=1, keepdims=True)
        out_ref[r] = (summed / total).astype(jnp.bfloat16)


def exchange(array, axis, k):
    size = lax.axis_size(axis)
    return lax.ppermute(array, axis, [(i, i ^ k) for i in range(size)])


def call(kernel, outs, in_specs, scratch=(), limit=None, cost=None):
    def run(*args):
        return pl.pallas_call(
            kernel,
            out_shape=outs,
            in_specs=in_specs,
            out_specs=jax.tree.map(lambda _: VMEM, outs),
            scratch_shapes=list(scratch),
            compiler_params=pltpu.CompilerParams(vmem_limit_bytes=limit),
            cost_estimate=cost,
        )(*args)

    return run


def in_hbm(array):
    return pltpu.with_memory_space_constraint(array, pltpu.HBM)


def start_order(groups):
    near = near_count(groups)
    far = list(range(near, groups))
    half = len(far) // 2
    return far[:half] + list(range(1, near)) + far[half:]


def near_count(groups):
    return min(4, groups)


def local(queries, own_cache, own_len, host_cache, host_len, page_plan, value_up):
    groups, n_sub = lax.axis_size("dp"), lax.axis_size("sub")
    requests, heads, width = queries.shape
    part = heads // n_sub
    slot_tokens = host_cache.shape[3]
    near = near_count(groups)
    far = groups - near
    near_rows = requests + near
    far_rows = far if far in (1, 2, 4) else -(-far // 8) * 8
    plan = page_plan.reshape(groups)
    lengths = host_len.reshape(groups)
    own_lengths = own_len.reshape(requests)
    own_keys = jnp.swapaxes(own_cache, 1, 2)
    host_keys = jnp.swapaxes(host_cache.reshape(groups, slot_tokens, width), 1, 2)

    targets = list(range(1, groups))
    packed = jax.ShapeDtypeStruct((heads * width // LANES, LANES), jnp.bfloat16)
    outgoing = call(
        functools.partial(pack_query_kernel, targets), [packed] * len(targets), [HBM, HBM],
        [pltpu.SMEM(plan.shape, plan.dtype), pltpu.VMEM(queries.shape, queries.dtype), pltpu.SemaphoreType.DMA((2,))],
        limit=PACK_LIMIT,
    )(in_hbm(plan), in_hbm(queries))
    order = start_order(groups)
    received = {k: exchange(outgoing[k - 1], "dp", k) for k in order}

    def message(rows):
        return jax.ShapeDtypeStruct((TILES * part * rows + part, LANES), jnp.bfloat16)

    def stage_shape(rows):
        return (TILES, heads * rows, LANES)

    def stages(rows):
        return [pltpu.VMEM(stage_shape(rows), jnp.float32), pltpu.VMEM((heads, LANES), jnp.float32)]

    def cost(slots):
        return pl.CostEstimate(
            flops=2 * slots * heads * slot_tokens * (width + DL),
            bytes_accessed=2 * slots * slot_tokens * width,
            transcendentals=slots * heads * slot_tokens,
        )

    cache, own_stage, table = call(
        functools.partial(own_kernel, near_rows),
        [
            jax.ShapeDtypeStruct(host_keys.shape, host_keys.dtype),
            jax.ShapeDtypeStruct(stage_shape(near_rows), jnp.float32),
            jax.ShapeDtypeStruct((heads, LANES), jnp.float32),
        ],
        [HBM] * 6,
        [
            pltpu.SMEM(plan.shape, plan.dtype),
            pltpu.SMEM(own_lengths.shape, own_lengths.dtype),
            pltpu.SMEM(lengths.shape, lengths.dtype),
            pltpu.VMEM(queries.shape, queries.dtype),
            pltpu.VMEM(own_keys.shape, own_keys.dtype),
            pltpu.SemaphoreType.DMA((5,)),
            pltpu.SemaphoreType.DMA((groups,)),
        ],
        limit=OWN_LIMIT,
        cost=cost(groups),
    )(*[in_hbm(x) for x in (plan, own_lengths, lengths, queries, own_keys, host_keys)])
    near_out = call(
        functools.partial(near_kernel, near, requests, near_rows, n_sub),
        [message(near_rows)] * n_sub,
        [SMEM] + [VMEM] * (3 + near - 1),
        stages(near_rows),
        limit=KERNEL_LIMIT,
        cost=cost(near - 1),
    )(lengths, cache, own_stage, table, *[received[k] for k in range(1, near)])
    far_out = call(
        functools.partial(far_kernel, near, far_rows, n_sub),
        [message(far_rows)] * n_sub,
        [SMEM] + [VMEM] * (1 + far),
        stages(far_rows),
        limit=KERNEL_LIMIT,
        cost=cost(far),
    )(lengths, cache, *[received[k] for k in range(near, groups)])
    sub_order = [k for k in range(2, n_sub)] + [1]
    near_in, far_in = {0: near_out[0]}, {0: far_out[0]}
    for k in sub_order:
        near_in[k] = exchange(near_out[k], "sub", k)
    for k in sub_order:
        far_in[k] = exchange(far_out[k], "sub", k)

    near_block, far_block = max(near_rows, 8), max(far_rows, 8)
    seats = n_sub * part
    back, own, side = call(
        functools.partial(lift_kernel, near, requests, near_rows, far_rows, n_sub, groups),
        [
            jax.ShapeDtypeStruct((groups, seats + part, LANES), jnp.bfloat16),
            jax.ShapeDtypeStruct((requests * seats, LANES), jnp.float32),
            jax.ShapeDtypeStruct((n_sub, part, LANES), jnp.float32),
        ],
        [VMEM] * (1 + 2 * n_sub),
        [
            pltpu.VMEM((part, n_sub * (near_block + far_block), DL), jnp.bfloat16),
            pltpu.VMEM(((near_block + far_block) * seats, LANES), jnp.float32),
        ],
        limit=12 << 20,
    )(value_up, *[near_in[k] for k in range(n_sub)], *[far_in[k] for k in range(n_sub)])
    back = lax.all_to_all(back, "dp", split_axis=0, concat_axis=0, tiled=True)
    return call(
        functools.partial(finish_kernel, requests, n_sub, groups),
        jax.ShapeDtypeStruct((requests, part, LANES), jnp.bfloat16),
        [VMEM] * 3,
        limit=4 << 20,
    )(back, own, side)


def solution(mesh):
    return jax.shard_map(
        local,
        mesh=mesh,
        in_specs=(
            P("dp", None, None),
            P("dp", "sub", None),
            P("dp", "sub"),
            P("dp", "sub", None, None, None),
            P("dp", "sub", None),
            P("dp", "sub", None),
            P("sub", None, None),
        ),
        out_specs=P("dp", "sub", None),
        check_vma=False,
    )
```
